128 devices in a mesh: ctx: 64 (over z, y, x), head: 2 (over core).
Axes of the slice: x: 4, y: 4, z: 4, core: 2. Of those that a mesh axis runs over, the one named last changes fastest.
Arguments:
- query: bfloat16 [24576, 6144], P(('ctx', 'head')), may hold values from -6 to 6
- key_in: bfloat16 [24576, 6144], P(('ctx', 'head')), may hold values from -6 to 6
- value: bfloat16 [24576, 6144], P(('ctx', 'head')), may hold values from -6 to 6
- cotangent: bfloat16 [24576, 6144], P(('ctx', 'head')), may hold values from -18 to 18
- decay_rate: float32 [48, 16], replicated, as said below
- residue: float32 [48, 16], replicated, may hold values from -2 to 2
Outputs:
- mixed: bfloat16 [24576, 6144], P(('ctx', 'head'))
- grad_query: bfloat16 [24576, 6144], P(('ctx', 'head'))
- grad_key: bfloat16 [24576, 6144], P(('ctx', 'head'))
- grad_value: bfloat16 [24576, 6144], P(('ctx', 'head'))
- residue_grad: float32 [48, 16], P('head')
The draws below stay inside these ranges and needn't reach their ends.
Inputs may be any that keep to these rules, and one draw needn't show every extreme that they name: `decay_rate`: positive decay rates of at most 1/30.
All inputs are finite; a program needn't handle non-finite values.
Results may differ from the reference program's by a relative error of at most 0.00105.
Values may be sent and summed in bfloat16 or wider, within the bound.
No kernel may reach another device: no remote copies, remote signals or barrier semaphores. Data moves between devices by JAX's collectives and lax.ppermute only.
A program may use at most 192 MiB of HBM per device.

```python
import math
import jax
import jax.numpy as jnp
from jax import lax

HEADS = 48
HEAD_DIM = 128
POLES = 16
D = 6144
LEN = 24576


def draw_decay_rate(key, part):
    flag_key, level_key = jax.random.split(key)
    slow_share = 0.5
    slow_head = jax.random.uniform(flag_key, (HEADS, 1), jnp.float32) < slow_share
    level_draw = jax.random.uniform(level_key, (HEADS, POLES), jnp.float32)
    slow_low = math.log(0.2 / LEN)
    slow_high = math.log(2.0 / LEN)
    fast_low = math.log(2.0 / LEN)
    fast_high = math.log(1.0 / 30.0)
    slow_rates = jnp.exp(slow_low + level_draw * (slow_high - slow_low))
    fast_rates = jnp.exp(fast_low + level_draw * (fast_high - fast_low))
    return jnp.where(slow_head, slow_rates, fast_rates).astype(jnp.float32)


def draw_cotangent(key, part):
    position = jnp.arange(LEN, dtype=jnp.float32) / max(LEN - 1, 1)
    envelope = 1.0 + 2.0 * position
    base_draw = jnp.clip(jax.random.normal(key, (LEN, HEADS * HEAD_DIM), jnp.float32), -6.0, 6.0)
    return (base_draw * envelope[:, None]).astype(jnp.bfloat16)


def shard_levels(stream_key, shape, cuts, least, high):
    loudness = 1.0
    for dim, blocks in cuts:
        heights = jax.random.uniform(jax.random.fold_in(jax.random.fold_in(stream_key, 6), dim), (blocks,), jnp.float32, least / len(cuts), high / len(cuts))
        loudness = loudness * jnp.repeat(jnp.exp(heights), shape[dim] // blocks).reshape((-1,) + (1,) * (len(shape) - 1 - dim))
    return loudness


def gaussian(own_key, shape, scale, most, cuts=(), kind=jnp.bfloat16):
    factor_of = shard_levels(own_key, shape, cuts, -0.22, 0.18) if cuts else 1.0
    array = jax.random.normal(own_key, shape, jnp.float32) * scale * factor_of
    return jnp.minimum(jnp.maximum(array, -most), most).astype(kind)


def setup_inputs(seed: int = 0) -> dict:
    arg_keys = jax.random.split(jax.random.key(seed), 7)
    return {
        "query": gaussian(arg_keys[0], (LEN, D), 1.0, 6.0, ((0, 128),)),
        "key_in": gaussian(arg_keys[1], (LEN, D), 1.0, 6.0, ((0, 128),)),
        "value": gaussian(arg_keys[2], (LEN, D), 1.0, 6.0, ((0, 128),)),
        "cotangent": draw_cotangent(jax.random.fold_in(arg_keys[6], 71), 0),
        "decay_rate": draw_decay_rate(jax.random.fold_in(arg_keys[6], 71), 0),
        "residue": gaussian(arg_keys[5], (HEADS, POLES), 0.35, 2.0, (), jnp.float32),
    }


def reference(query, key_in, value, cotangent, decay_rate, residue):
    norm_factor = jnp.sqrt(-jnp.expm1(-2.0 * decay_rate))
    coefficient = residue * norm_factor
    positions = jnp.arange(LEN, dtype=jnp.float32)
    fft_length = 2 * LEN

    def head_terms(head_index):
        first_col = (head_index * HEAD_DIM).astype(jnp.int32)

        def columns(source):
            return lax.dynamic_slice_in_dim(source, first_col, HEAD_DIM, 1).astype(jnp.float32)
        query_part = columns(query)
        key_part = columns(key_in)
        value_part = columns(value)
        cotan_part = columns(cotangent)
        rates = lax.dynamic_index_in_dim(decay_rate, head_index, 0, keepdims=False)
        coeffs = lax.dynamic_index_in_dim(coefficient, head_index, 0, keepdims=False)
        norms = lax.dynamic_index_in_dim(norm_factor, head_index, 0, keepdims=False)
        powers = jnp.exp(-rates[:, None] * positions[None, :])
        kernel = jnp.dot(coeffs, powers, precision=lax.Precision.HIGHEST)
        kernel_spec = jnp.fft.rfft(kernel, n=fft_length)
        product = key_part * value_part
        product_spec = jnp.fft.rfft(product, n=fft_length, axis=0)
        convolved = jnp.fft.irfft(product_spec * kernel_spec[:, None], n=fft_length, axis=0)[:LEN]
        mixed = (query_part * convolved).astype(jnp.bfloat16)
        grad_conv = cotan_part * query_part
        grad_query = (cotan_part * convolved).astype(jnp.bfloat16)
        grad_spec = jnp.fft.rfft(grad_conv[::-1], n=fft_length, axis=0)
        grad_product = jnp.fft.irfft(grad_spec * kernel_spec[:, None], n=fft_length, axis=0)[:LEN][::-1]
        grad_key = (grad_product * value_part).astype(jnp.bfloat16)
        grad_value = (grad_product * key_part).astype(jnp.bfloat16)
        lag_sums = jnp.fft.irfft(lax.optimization_barrier(jnp.sum(product_spec * grad_spec, axis=1)), n=fft_length)[:LEN][::-1]
        head_grad = norms * jnp.dot(powers, lag_sums, precision=lax.Precision.HIGHEST)
        return (mixed, grad_query, grad_key, grad_value, head_grad)
    outputs = lax.map(head_terms, jnp.arange(HEADS, dtype=jnp.int32))

    def to_rows(stacked):
        return jnp.transpose(stacked, (1, 0, 2)).reshape(LEN, HEADS * HEAD_DIM)
    residue_grad = outputs[4] / math.sqrt(float(LEN * HEAD_DIM))
    return (to_rows(outputs[0]), to_rows(outputs[1]), to_rows(outputs[2]), to_rows(outputs[3]), residue_grad)
```

```python
import math

import jax
import jax.numpy as jnp
from jax import lax
from jax.experimental import pallas as pl
from jax.experimental.pallas import tpu as pltpu
from jax.sharding import PartitionSpec as P

HEADS = 48
POLES = 16
WIDTH = 128
GROUP = 3
GROUPS = HEADS // GROUP
OWNERS = 8
ROWS = 64
F32 = jnp.float32
BF16 = jnp.bfloat16


def split(x):
    high = x.astype(BF16)
    return high, (x - high.astype(F32)).astype(BF16)


def mm(a, b):
    return jnp.dot(a, b, preferred_element_type=F32)


def mm_nt(a, b):
    return lax.dot_general(a, b, (((1,), (1,)), ((), ())), preferred_element_type=F32)


def head_of_row(shape, dim):
    return (lax.broadcasted_iota(jnp.int32, shape, dim) % 8) // 2


def states_kernel(rate_col, q_ref, k_ref, v_ref, c_ref, out_ref):
    rows = q_ref.shape[0]
    rate = rate_col[...][:, :1]
    step = lax.broadcasted_iota(jnp.int32, (ROWS, rows), 1).astype(F32)
    into = jnp.exp(-rate * step)
    ends = jnp.exp(-rate * (float(rows - 1) - step))
    into_hi, into_lo = split(into)
    ends_hi, ends_lo = split(ends)
    into_st = jnp.concatenate([into_hi, into_lo], 0)
    ends_st = jnp.concatenate([ends_hi, ends_lo], 0)
    owner_head = head_of_row((2 * ROWS, rows), 0)
    causal = lax.broadcasted_iota(jnp.int32, (rows, rows), 0) >= lax.broadcasted_iota(
        jnp.int32, (rows, rows), 1
    )
    fwd = jnp.zeros((ROWS, WIDTH), F32)
    bwd = jnp.zeros((ROWS, WIDTH), F32)
    near = jnp.zeros((ROWS, rows), F32)
    for h in range(GROUP):
        lanes = pl.ds(h * WIDTH, WIDTH)
        p_hi, p_lo = split(k_ref[:, lanes].astype(F32) * v_ref[:, lanes].astype(F32))
        g_hi, g_lo = split(c_ref[:, lanes].astype(F32) * q_ref[:, lanes].astype(F32))
        mine = owner_head == h
        zero = jnp.zeros((), BF16)
        in_h = jnp.where(mine, into_st, zero)
        en_h = jnp.where(mine, ends_st, zero)
        both = mm(en_h, p_hi)
        fwd += both[:ROWS] + both[ROWS:] + mm(en_h[:ROWS], p_lo)
        both = mm(in_h, g_hi)
        bwd += both[:ROWS] + both[ROWS:] + mm(in_h[:ROWS], g_lo)
        cross = mm_nt(g_hi, p_hi) + mm_nt(g_hi, p_lo) + mm_nt(g_lo, p_hi)
        x_hi, x_lo = split(jnp.where(causal, cross, 0.0))
        both = mm(in_h, x_hi)
        near += both[:ROWS] + both[ROWS:] + mm(in_h[:ROWS], x_lo)
    near_col = jnp.exp(rate * float(rows - 1)) * jnp.sum(near * ends, axis=1, keepdims=True)
    sub = lax.broadcasted_iota(jnp.int32, (ROWS, WIDTH), 0) % 8
    lane = lax.broadcasted_iota(jnp.int32, (ROWS, WIDTH), 1)
    near_rows = jnp.where(lane == sub, near_col, 0.0).reshape(OWNERS, 8, WIDTH).sum(axis=1)
    out_ref[:, :8, :] = fwd.reshape(OWNERS, 8, WIDTH)
    pad = jnp.broadcast_to(near_rows[:, None, :], (OWNERS, 8, WIDTH))
    row = lax.broadcasted_iota(jnp.int32, (OWNERS, 8, WIDTH), 1)
    out_ref[:, 8:, :] = jnp.where(row == 6, pad, bwd.reshape(OWNERS, 8, WIDTH))


def scan_kernel(place_ref, rate_ref, x_ref, out_ref, *, blocks, block_rows, scale):
    rate = rate_ref[...]
    sub = lax.broadcasted_iota(jnp.int32, (8, WIDTH), 0)
    lane = lax.broadcasted_iota(jnp.int32, (8, WIDTH), 1)
    over = jnp.exp(-rate * float(block_rows))
    zero = jnp.zeros((8, WIDTH), F32)

    def forward(e, carry):
        state, far, seen = carry
        adjoint = x_ref[e, 8:, :]
        out_ref[e, :8, :] = state
        return over * state + x_ref[e, :8, :], far + adjoint * state, seen + adjoint

    _, far, seen = lax.fori_loop(0, blocks, forward, (zero, zero, zero), unroll=8)
    near = jnp.where(lane == sub, jnp.broadcast_to(seen[6:7, :], (8, WIDTH)), 0.0)
    terms = jnp.where(sub < 6, jnp.exp(-rate) * far + near, 0.0)
    total = jnp.sum(terms, axis=1, keepdims=True)
    first = 2 * lax.rem(place_ref[0], OWNERS)

    def spread(h):
        hit = (sub == 2 * h + lane - first) & (lane >= first) & (lane < first + 2)
        return jnp.sum(jnp.where(hit, total * scale, 0.0), axis=0, keepdims=True)

    res0, res1, res2 = spread(0), spread(1), spread(2)
    pads = jnp.where(sub == 6, res0, res1)

    def backward(lap, state):
        e = blocks - 1 - lap
        out_ref[e, 6:8, :] = pads[6:8]
        out_ref[e, 8:, :] = jnp.where(sub == 6, res2, state)
        return over * state + x_ref[e, 8:, :]

    lax.fori_loop(0, blocks, backward, zero, unroll=8)


def toeplitz_kernel(rate_col, coef_col, rate_row, coef_row, q_ref, k_ref, v_ref, c_ref, conv_ref, grad_ref):
    rows = q_ref.shape[0]
    last = float(rows - 1)
    rate = rate_row[...].reshape(1, 3 * ROWS)
    coef = coef_row[...].reshape(1, 3 * ROWS)
    step = lax.broadcasted_iota(jnp.int32, (rows, 3 * ROWS), 0).astype(F32)
    third = lax.broadcasted_iota(jnp.int32, (rows, 3 * ROWS), 1) // ROWS
    owner_head = head_of_row((rows, 3 * ROWS), 1)

    def lefts(x):
        high, low = split(x)
        return jnp.where(third == 2, low, high)

    t_left = lefts(coef * jnp.exp(rate * (last - step)))
    u_left = lefts(jnp.exp(rate * step))
    rate_c = rate_col[...][:, :1]
    coef_c = coef_col[...][:, :1]
    across = lax.broadcasted_iota(jnp.int32, (ROWS, rows), 1).astype(F32)

    def rights(x):
        high, low = split(x)
        return jnp.concatenate([high, low, high], 0)

    t_right = rights(jnp.exp(-rate_c * (last - across)))
    u_right = rights(coef_c * jnp.exp(-rate_c * across))
    down = lax.broadcasted_iota(jnp.int32, (rows, rows), 0)
    right = lax.broadcasted_iota(jnp.int32, (rows, rows), 1)
    zero = jnp.zeros((), BF16)
    for h in range(GROUP):
        lanes = pl.ds(h * WIDTH, WIDTH)
        p_hi, p_lo = split(k_ref[:, lanes].astype(F32) * v_ref[:, lanes].astype(F32))
        g_hi, g_lo = split(c_ref[:, lanes].astype(F32) * q_ref[:, lanes].astype(F32))
        mine = owner_head == h
        t_hi, t_lo = split(jnp.where(down >= right, mm(jnp.where(mine, t_left, zero), t_right), 0.0))
        conv_ref[:, lanes] = mm(t_hi, p_hi) + mm(t_hi, p_lo) + mm(t_lo, p_hi)
        u_hi, u_lo = split(jnp.where(down <= right, mm(jnp.where(mine, u_left, zero), u_right), 0.0))
        grad_ref[:, lanes] = mm(u_hi, g_hi) + mm(u_hi, g_lo) + mm(u_lo, g_hi)


def output_kernel(
    rate_row, coef_row, s_ref, q_ref, k_ref, v_ref, c_ref, conv_ref, grad_ref,
    mixed_ref, gq_ref, gk_ref, gv_ref, res_ref,
):
    rows = q_ref.shape[0]
    rate = rate_row[...].reshape(1, 3 * ROWS)
    coef = coef_row[...].reshape(1, 3 * ROWS)
    step = lax.broadcasted_iota(jnp.int32, (rows, 3 * ROWS), 0).astype(F32)
    third = lax.broadcasted_iota(jnp.int32, (rows, 3 * ROWS), 1) // ROWS
    owner_head = head_of_row((rows, 3 * ROWS), 1)

    def lefts(x):
        high, low = split(x)
        return jnp.where(third == 2, low, high)

    inflow = lefts(coef * jnp.exp(-rate * (step + 1.0)))
    outflow = lefts(coef * jnp.exp(-rate * (float(rows) - step)))
    tile = s_ref[...]
    state = tile[:, :8, :].reshape(ROWS, WIDTH)
    later = tile[:, 8:, :].reshape(ROWS, WIDTH)

    def rights(x):
        high, low = split(x)
        return jnp.concatenate([high, low, high], 0)

    state_st = rights(state)
    later_st = rights(later)
    zero = jnp.zeros((), BF16)
    for h in range(GROUP):
        lanes = pl.ds(h * WIDTH, WIDTH)
        mine = owner_head == h
        conv = conv_ref[:, lanes] + mm(jnp.where(mine, inflow, zero), state_st)
        mixed_ref[:, lanes] = (q_ref[:, lanes].astype(F32) * conv).astype(BF16)
        gq_ref[:, lanes] = (c_ref[:, lanes].astype(F32) * conv).astype(BF16)
        grad = grad_ref[:, lanes] + mm(jnp.where(mine, outflow, zero), later_st)
        gk_ref[:, lanes] = (grad * v_ref[:, lanes].astype(F32)).astype(BF16)
        gv_ref[:, lanes] = (grad * k_ref[:, lanes].astype(F32)).astype(BF16)
    sub = lax.broadcasted_iota(jnp.int32, (8, WIDTH), 0)
    res = jnp.zeros((8, WIDTH), F32)
    for h in range(GROUP):
        spot = (6, 7, 14)[h]
        line = jnp.sum(tile[:, spot, :], axis=0, keepdims=True)
        res = jnp.where(sub == h, line, res)
    res_ref[0] = res


def by_owner(table):
    rows = table.reshape(GROUPS, GROUP, OWNERS, 2).transpose(0, 2, 1, 3)
    return jnp.pad(rows.reshape(GROUPS * OWNERS, 2 * GROUP), ((0, 0), (0, 2)))


def on_device(query, key_in, value, cotangent, decay_rate, residue):
    blocks = lax.axis_size("ctx") * lax.axis_size("head")
    place = lax.axis_index("ctx") * lax.axis_size("head") + lax.axis_index("head")
    rows, width = query.shape
    norm = jnp.sqrt(-jnp.expm1(-2.0 * decay_rate))
    rates = by_owner(decay_rate)
    coefs = by_owner(residue * norm)
    norms = by_owner(norm)
    rate_col = jnp.broadcast_to(rates.reshape(-1, 1), (GROUPS * ROWS, WIDTH))
    coef_col = jnp.broadcast_to(coefs.reshape(-1, 1), (GROUPS * ROWS, WIDTH))
    rate_row = jnp.tile(rates.reshape(GROUPS, 1, ROWS), (1, 1, 3))
    coef_row = jnp.tile(coefs.reshape(GROUPS, 1, ROWS), (1, 1, 3))
    own_rate = jnp.broadcast_to(lax.dynamic_index_in_dim(rates, place, 0, False)[:, None], (8, WIDTH))
    own_norm = jnp.broadcast_to(lax.dynamic_index_in_dim(norms, place, 0, False)[:, None], (8, WIDTH))

    wide = pl.BlockSpec((rows, GROUP * WIDTH), lambda g: (0, g))
    col = pl.BlockSpec((ROWS, WIDTH), lambda g: (g, 0))
    row = pl.BlockSpec((1, 1, 3 * ROWS), lambda g: (g, 0, 0))
    tile = pl.BlockSpec((OWNERS, 16, WIDTH), lambda g: (g, 0, 0))
    wide_bytes = 2 * rows * width
    states = pl.pallas_call(
        states_kernel,
        grid=(GROUPS,),
        in_specs=[col, wide, wide, wide, wide],
        out_specs=tile,
        out_shape=jax.ShapeDtypeStruct((GROUPS * OWNERS, 16, WIDTH), F32),
        cost_estimate=pl.CostEstimate(flops=10**10, bytes_accessed=5 * wide_bytes, transcendentals=0),
        name="states",
    )(rate_col, query, key_in, value, cotangent)
    gathered = lax.all_to_all(states, ("ctx", "head"), split_axis=0, concat_axis=0, tiled=True)

    conv, grad = pl.pallas_call(
        toeplitz_kernel,
        grid=(GROUPS,),
        in_specs=[col, col, row, row, wide, wide, wide, wide],
        out_specs=[wide, wide],
        out_shape=[jax.ShapeDtypeStruct((rows, width), F32)] * 2,
        cost_estimate=pl.CostEstimate(flops=10**10, bytes_accessed=8 * wide_bytes, transcendentals=0),
        name="toeplitz",
    )(rate_col, coef_col, rate_row, coef_row, query, key_in, value, cotangent)

    whole = pl.BlockSpec(memory_space=pltpu.VMEM)
    scanned = pl.pallas_call(
        lambda place_ref, rate_ref, norm_ref, x_ref, out_ref: scan_kernel(
            place_ref,
            rate_ref,
            x_ref,
            out_ref,
            blocks=blocks,
            block_rows=rows,
            scale=norm_ref[...][:, :1] / math.sqrt(float(rows * blocks * WIDTH)),
        ),
        in_specs=[pl.BlockSpec(memory_space=pltpu.SMEM), whole, whole, whole],
        out_specs=whole,
        out_shape=jax.ShapeDtypeStruct((blocks, 16, WIDTH), F32),
        cost_estimate=pl.CostEstimate(flops=10**6, bytes_accessed=2**21, transcendentals=0),
        name="scan",
    )(place.reshape(1), own_rate, own_norm, gathered)
    entering = lax.all_to_all(scanned, ("ctx", "head"), split_axis=0, concat_axis=0, tiled=True)

    out = jax.ShapeDtypeStruct((rows, width), BF16)
    mixed, grad_query, grad_key, grad_value, res = pl.pallas_call(
        output_kernel,
        grid=(GROUPS,),
        in_specs=[row, row, tile, wide, wide, wide, wide, wide, wide],
        out_specs=[wide, wide, wide, wide, pl.BlockSpec((1, 8, WIDTH), lambda g: (g, 0, 0))],
        out_shape=[out, out, out, out, jax.ShapeDtypeStruct((GROUPS, 8, WIDTH), F32)],
        cost_estimate=pl.CostEstimate(flops=10**9, bytes_accessed=12 * wide_bytes, transcendentals=0),
        name="outputs",
    )(rate_row, coef_row, entering, query, key_in, value, cotangent, conv, grad)
    half = GROUPS // lax.axis_size("head")
    mine = lax.dynamic_slice_in_dim(res, lax.axis_index("head") * half, half, 0)
    residue_grad = mine[:, :GROUP, :POLES].reshape(half * GROUP, POLES)
    return mixed, grad_query, grad_key, grad_value, residue_grad


def solution(mesh):
    wide = P(("ctx", "head"), None)
    return jax.shard_map(
        on_device,
        mesh=mesh,
        in_specs=(wide, wide, wide, wide, P(), P()),
        out_specs=(wide, wide, wide, wide, P("head", None)),
        check_vma=False,
    )
```

```python
import functools
import math

import jax
import jax.numpy as jnp
from jax import lax
from jax.experimental import pallas as pl
from jax.experimental.pallas import tpu as pltpu
from jax.sharding import PartitionSpec as P

HEADS = 48
POLES = 16
WIDTH = 128
GROUP = 3
GROUPS = HEADS // GROUP
PACK = 4
OWNERS = 8
UNITS = 2 * GROUP
CHUNK = 64
BATCH = {"states": 4, "near": 4, "local": 4, "outputs": 4}
F32 = jnp.float32
BF16 = jnp.bfloat16
VMEM_LIMIT = 12 * 2**20


def split(x):
    high = x.astype(BF16)
    return high, (x - high.astype(F32)).astype(BF16)


def iota(shape, dim):
    return lax.broadcasted_iota(jnp.int32, shape, dim)


def mm(a, b):
    return jnp.dot(a, b, preferred_element_type=F32)


def mm_nt(a, b):
    return lax.dot_general(a, b, (((1,), (1,)), ((), ())), preferred_element_type=F32)


def mm_tn(a, b):
    return lax.dot_general(a, b, (((0,), (0,)), ((), ())), preferred_element_type=F32)


def stacked(x, parts=(0, 1, 0)):
    both = split(x)
    return jnp.concatenate([both[p] for p in parts], 0)


def column(table, head, first=0, count=POLES):
    hit = iota((count, HEADS), 1) == head
    return jnp.sum(jnp.where(hit, table[first : first + count, :], 0.0), axis=1, keepdims=True)


def product(a_ref, b_ref, lanes):
    return split(a_ref[:, lanes].astype(F32) * b_ref[:, lanes].astype(F32))


def lanes_of(at, h):
    return pl.ds(pl.multiple_of((at * GROUP + h) * WIDTH, WIDTH), WIDTH)


def each_batch(batch, body):
    def lap(n, _):
        body([(n * batch + j, pl.program_id(0) * PACK + n * batch + j) for j in range(batch)])
        return 0

    lax.fori_loop(0, PACK // batch, lap, 0)


def sublane_of(owner, unit):
    return lax.rem(owner + 8 - unit, 8)


def read_unit(ref, at, u, first):
    sub = iota((8, WIDTH), 0)
    tile = jnp.zeros((8, WIDTH), F32)
    for owner in range(OWNERS):
        tile = jnp.where(sub == (owner - u) % 8, ref[at * OWNERS + owner, pl.ds(first, 8), :], tile)
    return tile


def read_head(ref, at, h, first):
    return jnp.concatenate([read_unit(ref, at, 2 * h, first), read_unit(ref, at, 2 * h + 1, first)], 0)


def states_kernel(rate_ref, q_ref, k_ref, v_ref, c_ref, out_ref):
    rows = q_ref.shape[0]
    spot = iota((POLES, rows), 1).astype(F32)
    sub = iota((8, WIDTH), 0)

    def batch(groups):
        for at, number in groups:
            ahead, back = [], []
            for h in range(GROUP):
                lanes = lanes_of(at, h)
                rate = column(rate_ref, number * GROUP + h)

                def state(weights, high, low):
                    w_hi, w_lo = split(weights)
                    both = mm(jnp.concatenate([w_hi, w_lo], 0), high)
                    return both[:POLES] + both[POLES:] + mm(w_hi, low)

                fwd = state(jnp.exp(-rate * (float(rows - 1) - spot)), *product(k_ref, v_ref, lanes))
                bwd = state(jnp.exp(-rate * spot), *product(c_ref, q_ref, lanes))
                ahead += [fwd[:8], fwd[8:]]
                back += [bwd[:8], bwd[8:]]
            for owner in range(OWNERS):
                for first, units in ((0, ahead), (8, back)):
                    tile = jnp.zeros((8, WIDTH), F32)
                    for u in range(UNITS):
                        tile = jnp.where(sub == (owner - u) % 8, units[u], tile)
                    out_ref[at * OWNERS + owner, first : first + 8, :] = tile

    each_batch(BATCH["states"], batch)


def near_kernel(
    rate_ref, norm_ref, q_ref, k_ref, v_ref, c_ref,
    out_ref, part_ref, ph_ref, pl_ref, gh_ref, gl_ref, *, scale,
):
    rows = q_ref.shape[0]
    chunks = rows // CHUNK
    step = pl.program_id(0)
    spot = iota((POLES, chunks * CHUNK), 1)
    local = (spot % CHUNK).astype(F32)
    causal = iota((CHUNK, CHUNK), 0) >= iota((CHUNK, CHUNK), 1)
    lane = iota((8, WIDTH), 1)
    sub = iota((8, WIDTH), 0)
    wide = iota((POLES, WIDTH), 1) % POLES == iota((POLES, WIDTH), 0)

    @pl.when(step == 0)
    def _():
        out_ref[...] = jnp.zeros_like(out_ref)

    def part_states(weights, high, low):
        w_hi, w_lo = split(weights)
        zero = jnp.zeros((), BF16)
        w_hi = jnp.concatenate([jnp.where(spot // CHUNK == c, w_hi, zero) for c in range(chunks)], 0)
        w_lo = jnp.concatenate([jnp.where(spot // CHUNK == c, w_lo, zero) for c in range(chunks)], 0)
        both = mm(jnp.concatenate([w_hi, w_lo], 0), high)
        return both[: chunks * POLES] + both[chunks * POLES :] + mm(w_hi, low)

    def batch(groups):
        heads = [(at * GROUP + h, number * GROUP + h, lanes_of(at, h)) for at, number in groups for h in range(GROUP)]
        crosses, moves, parts, total = [], [], [], out_ref[...]
        for at, head, lanes in heads:
            p_hi, p_lo = product(k_ref, v_ref, lanes)
            g_hi, g_lo = product(c_ref, q_ref, lanes)
            ph_ref[:, lanes], pl_ref[:, lanes] = p_hi, p_lo
            gh_ref[:, lanes], gl_ref[:, lanes] = g_hi, g_lo
            rate = column(rate_ref, head)
            f = part_states(jnp.exp(-rate * (float(CHUNK - 1) - local)), p_hi, p_lo)
            b = part_states(jnp.exp(-rate * local), g_hi, g_lo)
            part_ref[at, 0], part_ref[at, 1] = f, b
            parts.append((f, b))
            cross = jnp.zeros((2 * CHUNK, 2 * CHUNK), F32)
            for c in range(chunks):
                span = slice(c * CHUNK, (c + 1) * CHUNK)
                left = jnp.concatenate([g_hi[span], g_lo[span]], 0)
                right = jnp.concatenate([p_hi[span], p_lo[span]], 0)
                cross += mm_nt(left, right)
            cross = cross[:CHUNK, :CHUNK] + (cross[:CHUNK, CHUNK:] + cross[CHUNK:, :CHUNK])
            crosses.append(stacked(jnp.where(causal, cross, 0.0)))
        for cross, (_, head, _) in zip(crosses, heads):
            into_hi, into_lo = split(jnp.exp(-column(rate_ref, head) * local))
            moves.append(mm(jnp.where(spot // CHUNK == 2, into_lo, into_hi), cross))
        for moved, (f, b), (_, head, _) in zip(moves, parts, heads):
            rate = column(rate_ref, head)
            over = jnp.exp(-rate * float(CHUNK))
            ends = jnp.exp(-rate * (float(CHUNK - 1) - local[:, :CHUNK]))
            near = jnp.exp(rate * float(CHUNK - 1)) * jnp.sum(moved * ends, axis=1, keepdims=True)
            state = f[:POLES]
            far = jnp.zeros((POLES, WIDTH), F32)
            for c in range(1, chunks):
                far += b[c * POLES : (c + 1) * POLES] * state
                state = f[c * POLES : (c + 1) * POLES] + over * state
            near += jnp.exp(-rate) * jnp.sum(far, axis=1, keepdims=True)
            near *= column(norm_ref, head) * scale
            line = jnp.sum(jnp.where(wide, near, 0.0), axis=0, keepdims=True)
            total += jnp.where((sub == head // 8) & (lane // POLES == head % 8), line, 0.0)
        out_ref[...] = total

    each_batch(BATCH["near"], batch)


def local_kernel(rate_ref, coef_ref, part_ref, ph_ref, pl_ref, gh_ref, gl_ref, conv_ref, grad_ref):
    chunks = ph_ref.shape[0] // CHUNK
    wide = 3 * CHUNK + 3 * POLES
    lane_t = iota((POLES, wide), 1)
    hit = (lane_t - 3 * CHUNK) % POLES == iota((POLES, wide), 0)
    ramp = (lane_t % CHUNK).astype(F32)
    here = iota((POLES, CHUNK), 1).astype(F32)
    down = iota((CHUNK, wide), 0)
    lane = iota((CHUNK, wide), 1)
    low_part = ((lane >= 2 * CHUNK) & (lane < 3 * CHUNK)) | (lane >= 3 * CHUNK + 2 * POLES)

    def batch(groups):
        heads = [(at * GROUP + h, number * GROUP + h, lanes_of(at, h)) for at, number in groups for h in range(GROUP)]
        done = []
        for side, (high_ref, low_ref, out_ref) in enumerate(((ph_ref, pl_ref, conv_ref), (gh_ref, gl_ref, grad_ref))):
            flip = (lambda x: float(CHUNK - 1) - x) if side else (lambda x: x)
            keep = ((down <= lane % CHUNK) if side else (down >= lane % CHUNK)) | (lane >= 3 * CHUNK)
            tables = []
            for _, head, _ in heads:
                rate = column(rate_ref, head)
                left = column(coef_ref, head) * jnp.exp(-rate * flip(here))
                right = jnp.where(
                    lane_t < 3 * CHUNK, jnp.exp(rate * flip(ramp)), jnp.where(hit, jnp.exp(-rate), 0.0)
                )
                table = mm_tn(stacked(left, (0, 0, 1)), stacked(right))
                t_hi, t_lo = split(jnp.where(keep, table, 0.0))
                tables.append(jnp.where(low_part, t_lo, t_hi))
            for table, (at, head, lanes) in zip(tables, heads):
                over = jnp.exp(-column(rate_ref, head) * float(CHUNK))
                state = jnp.zeros((POLES, WIDTH), F32)
                for c in reversed(range(chunks)) if side else range(chunks):
                    span = slice(c * CHUNK, (c + 1) * CHUNK)
                    s_hi, s_lo = split(state)
                    high, low = high_ref[span, lanes], low_ref[span, lanes]
                    source = jnp.concatenate([high, low, high, s_hi, s_lo, s_hi], 0)
                    done.append((out_ref, span, lanes, mm(table, source)))
                    state = part_ref[at, side, c * POLES : (c + 1) * POLES] + over * state
        for out_ref, span, lanes, value in done:
            out_ref[span, lanes] = value

    each_batch(BATCH["local"], batch)


def scan_kernel(place_ref, rate_ref, norm_ref, near_ref, x_ref, out_ref, *, block_rows, scale):
    blocks = x_ref.shape[0]
    group = place_ref[0] // OWNERS
    owner = lax.rem(place_ref[0], OWNERS)
    sub = iota((8, WIDTH), 0)
    lane = iota((8, WIDTH), 1)
    zero = jnp.zeros((8, WIDTH), F32)

    def own(table):
        rows = zero
        for u in range(UNITS):
            rows = jnp.where(
                sub == sublane_of(owner, u), column(table, group * GROUP + u // 2, 8 * (u % 2), 8), rows
            )
        return rows

    rate = own(rate_ref)
    over = jnp.exp(-rate * float(block_rows))

    def forward(e, carry):
        state, far = carry
        out_ref[e, :8, :] = state
        return over * state + x_ref[e, :8, :], far + x_ref[e, 8:, :] * state

    _, far = lax.fori_loop(0, blocks, forward, (zero, zero), unroll=8)
    far = jnp.sum(far * jnp.exp(-rate), axis=1, keepdims=True) * own(norm_ref) * scale
    total = near_ref[...]
    for u in range(UNITS):
        at = sublane_of(owner, u)
        head = group * GROUP + u // 2
        value = jnp.sum(jnp.where(sub == at, far, 0.0), axis=0, keepdims=True)
        spot = POLES * lax.rem(head, 8) + 8 * (u % 2) + at
        total += jnp.where((sub == head // 8) & (lane == spot), value, 0.0)
    used = zero == 0.0
    pads = [[zero, zero], [zero, zero]]
    for u, side, line in ((6, 0, 0), (7, 0, 1), (6, 1, 2), (7, 1, None)):
        at = sub == sublane_of(owner, u)
        used = used & ~at
        if line is not None:
            for k in range(2):
                pads[k][side] = jnp.where(at, total[3 * k + line : 3 * k + line + 1], pads[k][side])

    def backward(lap, state):
        for k in (1, 0):
            e = blocks - 2 - 2 * lap + k
            out_ref[e, :8, :] = jnp.where(used, out_ref[e, :8, :], pads[k][0])
            out_ref[e, 8:, :] = jnp.where(used, state, pads[k][1])
            state = over * state + x_ref[e, 8:, :]
        return state

    lax.fori_loop(0, blocks // 2, backward, zero, unroll=4)


def output_kernel(
    rate_ref, coef_ref, s_ref, q_ref, k_ref, v_ref, c_ref, conv_ref, grad_ref,
    mixed_ref, gq_ref, gk_ref, gv_ref, res_ref, sums,
):
    rows = q_ref.shape[0]
    spot = iota((POLES, rows), 1).astype(F32)
    sub = iota((8, WIDTH), 0)
    step = pl.program_id(0)

    @pl.when(step == 0)
    def _():
        sums[...] = jnp.zeros_like(sums)

    res = sums[...]
    for at in range(PACK):
        for u, first, line in ((6, 0, 0), (7, 0, 1), (6, 8, 2)):
            value = jnp.zeros((1, WIDTH), F32)
            for owner in range(OWNERS):
                row = first + (owner - u) % 8
                value += s_ref[at * OWNERS + owner, row : row + 1, :]
            res += jnp.where(sub == line, value, 0.0)
    sums[...] = res

    @pl.when(step == pl.num_programs(0) - 1)
    def _():
        half = HEADS // 2
        wide = iota((POLES, WIDTH), 1) % POLES == iota((POLES, WIDTH), 0)
        source = iota((WIDTH, half), 0) // POLES
        target = iota((WIDTH, half), 1)
        out = jnp.zeros((POLES, half), F32)
        for line in range(half * POLES // WIDTH):
            high, low = split(jnp.where(wide, sums[line : line + 1, :], 0.0))
            pick = jnp.where(target == 8 * line + source, 1.0, 0.0).astype(BF16)
            out += mm(high, pick) + mm(low, pick)
        res_ref[...] = out

    def group(at, number):
        done = []
        for h in range(GROUP):
            lanes = lanes_of(at, h)
            head = number * GROUP + h
            rate = column(rate_ref, head)
            coef = column(coef_ref, head)
            state = read_head(s_ref, at, h, 0)
            later = read_head(s_ref, at, h, 8)
            inflow = stacked(coef * jnp.exp(-rate * (spot + 1.0)), (0, 0, 1))
            outflow = stacked(coef * jnp.exp(-rate * (float(rows) - spot)), (0, 0, 1))
            conv = conv_ref[:, lanes] + mm_tn(inflow, stacked(state))
            done.append((mixed_ref, lanes, (q_ref[:, lanes].astype(F32) * conv).astype(BF16)))
            done.append((gq_ref, lanes, (c_ref[:, lanes].astype(F32) * conv).astype(BF16)))
            grad = grad_ref[:, lanes] + mm_tn(outflow, stacked(later))
            done.append((gk_ref, lanes, (grad * v_ref[:, lanes].astype(F32)).astype(BF16)))
            done.append((gv_ref, lanes, (grad * k_ref[:, lanes].astype(F32)).astype(BF16)))
        for ref, lanes, value in done:
            ref[:, lanes] = value

    each_batch(BATCH["outputs"], lambda groups: [group(*g) for g in groups])


def on_device(query, key_in, value, cotangent, decay_rate, residue):
    blocks = lax.axis_size("ctx") * lax.axis_size("head")
    place = lax.axis_index("ctx") * lax.axis_size("head") + lax.axis_index("head")
    rows, width = query.shape
    chunks = rows // CHUNK
    steps = GROUPS // PACK
    scale = 1.0 / math.sqrt(float(rows * blocks * WIDTH))
    rates = decay_rate.T
    norms = jnp.sqrt(-jnp.expm1(-2.0 * rates))
    coefs = residue.T * norms

    wide = pl.BlockSpec((rows, PACK * GROUP * WIDTH), lambda g: (0, g))
    small = pl.BlockSpec((POLES, HEADS), lambda g: (0, 0))
    fixed = pl.BlockSpec((8, WIDTH), lambda g: (0, 0))
    tile = pl.BlockSpec((PACK * OWNERS, 16, WIDTH), lambda g: (g, 0, 0))
    part = pl.BlockSpec((PACK * GROUP, 2, chunks * POLES, WIDTH), lambda g: (g, 0, 0, 0))
    wide_bytes = 2 * rows * width
    out16 = jax.ShapeDtypeStruct((rows, width), BF16)
    out32 = jax.ShapeDtypeStruct((rows, width), F32)
    line = jax.ShapeDtypeStruct((8, WIDTH), F32)
    tiles = jax.ShapeDtypeStruct((GROUPS * OWNERS, 16, WIDTH), F32)
    part_out = jax.ShapeDtypeStruct((HEADS, 2, chunks * POLES, WIDTH), F32)

    def call(kernel, name, grid, in_specs, out_specs, out_shape, passes, limit=None, scratch=(), **fixed_args):
        return pl.pallas_call(
            functools.partial(kernel, **fixed_args),
            grid=grid,
            in_specs=in_specs,
            out_specs=out_specs,
            out_shape=out_shape,
            scratch_shapes=scratch,
            cost_estimate=pl.CostEstimate(
                flops=10**9 * passes, bytes_accessed=passes * wide_bytes, transcendentals=0
            ),
            compiler_params=pltpu.CompilerParams(vmem_limit_bytes=limit),
            name=name,
        )

    gates = (query, key_in, value, cotangent)
    states = call(states_kernel, "states", (steps,), [small, wide, wide, wide, wide], tile, tiles, 4)(rates, *gates)
    gathered = lax.all_to_all(states, ("ctx", "head"), split_axis=0, concat_axis=0, tiled=True)

    near, parts, *products = call(
        near_kernel,
        "near",
        (steps,),
        [small, small, wide, wide, wide, wide],
        [fixed, part, wide, wide, wide, wide],
        [line, part_out, out16, out16, out16, out16],
        9,
        scale=scale,
    )(rates, norms, *gates)

    conv, grad = call(
        local_kernel,
        "local",
        (steps,),
        [small, small, part, wide, wide, wide, wide],
        [wide, wide],
        [out32, out32],
        9,
    )(rates, coefs, parts, *products)

    whole = pl.BlockSpec(memory_space=pltpu.VMEM)
    scanned = call(
        scan_kernel,
        "scan",
        (),
        [pl.BlockSpec(memory_space=pltpu.SMEM), whole, whole, whole, whole],
        whole,
        tiles,
        1,
        limit=VMEM_LIMIT,
        block_rows=rows,
        scale=scale,
    )(place.reshape(1), rates, norms, near, gathered)
    entering = lax.all_to_all(scanned, ("ctx", "head"), split_axis=0, concat_axis=0, tiled=True)

    *outs, res = call(
        output_kernel,
        "outputs",
        (steps,),
        [small, small, tile, wide, wide, wide, wide, wide, wide],
        [wide, wide, wide, wide, pl.BlockSpec((POLES, HEADS // 2), lambda g: (0, 0))],
        [out16, out16, out16, out16, jax.ShapeDtypeStruct((POLES, HEADS // 2), F32)],
        12,
        scratch=[pltpu.VMEM((8, WIDTH), F32)],
    )(rates, coefs, entering, *gates, conv, grad)
    return (*outs, res.T)


def solution(mesh):
    wide = P(("ctx", "head"), None)
    return jax.shard_map(
        on_device,
        mesh=mesh,
        in_specs=(wide, wide, wide, wide, P(), P()),
        out_specs=(wide, wide, wide, wide, P("head", None)),
        check_vma=False,
    )
```

```python
import functools
import math

import jax
import jax.numpy as jnp
from jax import lax
from jax.experimental import pallas as pl
from jax.experimental.pallas import tpu as pltpu
from jax.sharding import PartitionSpec as P

HEADS = 48
POLES = 16
WIDTH = 128
GROUP = 3
GROUPS = HEADS // GROUP
PACK = 4
OWNERS = 8
UNITS = 2 * GROUP
CHUNK = 64
BATCH = {"states": 4, "near": 4, "local": 4, "outputs": 4}
F32 = jnp.float32
BF16 = jnp.bfloat16
VMEM_LIMIT = 12 * 2**20
OUT_LIMIT = 51 * 2**20
LOCAL_LIMIT = None
OUT_PACK = 4


def split(x):
    high = x.astype(BF16)
    return high, (x - high.astype(F32)).astype(BF16)


def iota(shape, dim):
    return lax.broadcasted_iota(jnp.int32, shape, dim)


def mm(a, b):
    return jnp.dot(a, b, preferred_element_type=F32)


def mm_nt(a, b):
    return lax.dot_general(a, b, (((1,), (1,)), ((), ())), preferred_element_type=F32)


def mm_tn(a, b):
    return lax.dot_general(a, b, (((0,), (0,)), ((), ())), preferred_element_type=F32)


def stacked(x, parts=(0, 1, 0)):
    both = split(x)
    return jnp.concatenate([both[p] for p in parts], 0)


def column(table, head, first=0, count=POLES):
    hit = iota((count, HEADS), 1) == head
    return jnp.sum(jnp.where(hit, table[first : first + count, :], 0.0), axis=1, keepdims=True)


def product(a_ref, b_ref, lanes):
    return split(a_ref[:, lanes].astype(F32) * b_ref[:, lanes].astype(F32))


def lanes_of(at, h):
    return pl.ds(pl.multiple_of((at * GROUP + h) * WIDTH, WIDTH), WIDTH)


def each_batch(batch, body, pack=PACK):
    def lap(n, _):
        body([(n * batch + j, pl.program_id(0) * pack + n * batch + j) for j in range(batch)])
        return 0

    lax.fori_loop(0, pack // batch, lap, 0)


def sublane_of(owner, unit):
    return lax.rem(owner + 8 - unit, 8)


def read_unit(ref, at, u, first):
    sub = iota((8, WIDTH), 0)
    tile = jnp.zeros((8, WIDTH), F32)
    for owner in range(OWNERS):
        tile = jnp.where(sub == (owner - u) % 8, ref[at * OWNERS + owner, pl.ds(first, 8), :], tile)
    return tile


def read_head(ref, at, h, first):
    return jnp.concatenate([read_unit(ref, at, 2 * h, first), read_unit(ref, at, 2 * h + 1, first)], 0)


def states_kernel(rate_ref, q_ref, k_ref, v_ref, c_ref, out_ref):
    rows = q_ref.shape[0]
    spot = iota((POLES, rows), 1).astype(F32)
    sub = iota((8, WIDTH), 0)

    def batch(groups):
        for at, number in groups:
            ahead, back = [], []
            for h in range(GROUP):
                lanes = lanes_of(at, h)
                rate = column(rate_ref, number * GROUP + h)

                def state(weights, high, low):
                    w_hi, w_lo = split(weights)
                    both = mm(jnp.concatenate([w_hi, w_lo], 0), high)
                    return both[:POLES] + both[POLES:] + mm(w_hi, low)

                fwd = state(jnp.exp(-rate * (float(rows - 1) - spot)), *product(k_ref, v_ref, lanes))
                bwd = state(jnp.exp(-rate * spot), *product(c_ref, q_ref, lanes))
                ahead += [fwd[:8], fwd[8:]]
                back += [bwd[:8], bwd[8:]]
            for owner in range(OWNERS):
                for first, units in ((0, ahead), (8, back)):
                    tile = jnp.zeros((8, WIDTH), F32)
                    for u in range(UNITS):
                        tile = jnp.where(sub == (owner - u) % 8, units[u], tile)
                    out_ref[at * OWNERS + owner, first : first + 8, :] = tile

    each_batch(BATCH["states"], batch)


def near_kernel(
    rate_ref, norm_ref, q_ref, k_ref, v_ref, c_ref,
    out_ref, part_ref, ph_ref, pl_ref, gh_ref, gl_ref, *, scale,
):
    rows = q_ref.shape[0]
    chunks = rows // CHUNK
    step = pl.program_id(0)
    spot = iota((POLES, chunks * CHUNK), 1)
    local = (spot % CHUNK).astype(F32)
    causal = iota((CHUNK, CHUNK), 0) >= iota((CHUNK, CHUNK), 1)
    lane = iota((8, WIDTH), 1)
    sub = iota((8, WIDTH), 0)
    wide = iota((POLES, WIDTH), 1) % POLES == iota((POLES, WIDTH), 0)

    @pl.when(step == 0)
    def _():
        out_ref[...] = jnp.zeros_like(out_ref)

    def part_states(weights, high, low):
        w_hi, w_lo = split(weights)
        zero = jnp.zeros((), BF16)
        w_hi = jnp.concatenate([jnp.where(spot // CHUNK == c, w_hi, zero) for c in range(chunks)], 0)
        w_lo = jnp.concatenate([jnp.where(spot // CHUNK == c, w_lo, zero) for c in range(chunks)], 0)
        both = mm(jnp.concatenate([w_hi, w_lo], 0), high)
        return both[: chunks * POLES] + both[chunks * POLES :] + mm(w_hi, low)

    def batch(groups):
        heads = [(at * GROUP + h, number * GROUP + h, lanes_of(at, h)) for at, number in groups for h in range(GROUP)]
        crosses, moves, parts, total = [], [], [], out_ref[...]
        for at, head, lanes in heads:
            p_hi, p_lo = product(k_ref, v_ref, lanes)
            g_hi, g_lo = product(c_ref, q_ref, lanes)
            ph_ref[:, lanes], pl_ref[:, lanes] = p_hi, p_lo
            gh_ref[:, lanes], gl_ref[:, lanes] = g_hi, g_lo
            rate = column(rate_ref, head)
            f = part_states(jnp.exp(-rate * (float(CHUNK - 1) - local)), p_hi, p_lo)
            b = part_states(jnp.exp(-rate * local), g_hi, g_lo)
            part_ref[at, 0], part_ref[at, 1] = f, b
            parts.append((f, b))
            cross = jnp.zeros((2 * CHUNK, 2 * CHUNK), F32)
            for c in range(chunks):
                span = slice(c * CHUNK, (c + 1) * CHUNK)
                left = jnp.concatenate([g_hi[span], g_lo[span]], 0)
                right = jnp.concatenate([p_hi[span], p_lo[span]], 0)
                cross += mm_nt(left, right)
            cross = cross[:CHUNK, :CHUNK] + (cross[:CHUNK, CHUNK:] + cross[CHUNK:, :CHUNK])
            crosses.append(stacked(jnp.where(causal, cross, 0.0)))
        for cross, (_, head, _) in zip(crosses, heads):
            into_hi, into_lo = split(jnp.exp(-column(rate_ref, head) * local))
            moves.append(mm(jnp.where(spot // CHUNK == 2, into_lo, into_hi), cross))
        for moved, (f, b), (_, head, _) in zip(moves, parts, heads):
            rate = column(rate_ref, head)
            over = jnp.exp(-rate * float(CHUNK))
            ends = jnp.exp(-rate * (float(CHUNK - 1) - local[:, :CHUNK]))
            near = jnp.exp(rate * float(CHUNK - 1)) * jnp.sum(moved * ends, axis=1, keepdims=True)
            state = f[:POLES]
            far = jnp.zeros((POLES, WIDTH), F32)
            for c in range(1, chunks):
                far += b[c * POLES : (c + 1) * POLES] * state
                state = f[c * POLES : (c + 1) * POLES] + over * state
            near += jnp.exp(-rate) * jnp.sum(far, axis=1, keepdims=True)
            near *= column(norm_ref, head) * scale
            line = jnp.sum(jnp.where(wide, near, 0.0), axis=0, keepdims=True)
            total += jnp.where((sub == head // 8) & (lane // POLES == head % 8), line, 0.0)
        out_ref[...] = total

    each_batch(BATCH["near"], batch)


def local_kernel(rate_ref, coef_ref, part_ref, ph_ref, pl_ref, gh_ref, gl_ref, conv_ref, grad_ref):
    chunks = ph_ref.shape[0] // CHUNK
    wide = 3 * CHUNK + 3 * POLES
    lane_t = iota((POLES, wide), 1)
    hit = (lane_t - 3 * CHUNK) % POLES == iota((POLES, wide), 0)
    ramp = (lane_t % CHUNK).astype(F32)
    here = iota((POLES, CHUNK), 1).astype(F32)
    down = iota((CHUNK, wide), 0)
    lane = iota((CHUNK, wide), 1)
    low_part = ((lane >= 2 * CHUNK) & (lane < 3 * CHUNK)) | (lane >= 3 * CHUNK + 2 * POLES)

    def batch(groups):
        heads = [(at * GROUP + h, number * GROUP + h, lanes_of(at, h)) for at, number in groups for h in range(GROUP)]
        done = []
        for side, (high_ref, low_ref, out_ref) in enumerate(((ph_ref, pl_ref, conv_ref), (gh_ref, gl_ref, grad_ref))):
            flip = (lambda x: float(CHUNK - 1) - x) if side else (lambda x: x)
            keep = ((down <= lane % CHUNK) if side else (down >= lane % CHUNK)) | (lane >= 3 * CHUNK)
            tables = []
            for _, head, _ in heads:
                rate = column(rate_ref, head)
                left = column(coef_ref, head) * jnp.exp(-rate * flip(here))
                right = jnp.where(
                    lane_t < 3 * CHUNK, jnp.exp(rate * flip(ramp)), jnp.where(hit, jnp.exp(-rate), 0.0)
                )
                table = mm_tn(stacked(left, (0, 0, 1)), stacked(right))
                t_hi, t_lo = split(jnp.where(keep, table, 0.0))
                tables.append(jnp.where(low_part, t_lo, t_hi))
            for table, (at, head, lanes) in zip(tables, heads):
                over = jnp.exp(-column(rate_ref, head) * float(CHUNK))
                state = jnp.zeros((POLES, WIDTH), F32)
                for c in reversed(range(chunks)) if side else range(chunks):
                    span = slice(c * CHUNK, (c + 1) * CHUNK)
                    s_hi, s_lo = split(state)
                    high, low = high_ref[span, lanes], low_ref[span, lanes]
                    source = jnp.concatenate([high, low, high, s_hi, s_lo, s_hi], 0)
                    done.append((out_ref, span, lanes, mm(table, source)))
                    state = part_ref[at, side, c * POLES : (c + 1) * POLES] + over * state
        for out_ref, span, lanes, value in done:
            out_ref[span, lanes] = value

    each_batch(BATCH["local"], batch)


def scan_kernel(place_ref, rate_ref, norm_ref, near_hbm, x_ref, out_ref, near_ref, arrived, *, block_rows, scale):
    fetch = pltpu.make_async_copy(near_hbm, near_ref, arrived)
    fetch.start()
    blocks = x_ref.shape[0]
    group = place_ref[0] // OWNERS
    owner = lax.rem(place_ref[0], OWNERS)
    sub = iota((8, WIDTH), 0)
    lane = iota((8, WIDTH), 1)
    zero = jnp.zeros((8, WIDTH), F32)

    def own(table):
        rows = zero
        for u in range(UNITS):
            rows = jnp.where(
                sub == sublane_of(owner, u), column(table, group * GROUP + u // 2, 8 * (u % 2), 8), rows
            )
        return rows

    rate = own(rate_ref)
    over = jnp.exp(-rate * float(block_rows))

    def both(e, carry):
        state, adjoint, far = carry
        back = blocks - 1 - e
        out_ref[e, :8, :] = state
        out_ref[back, 8:, :] = adjoint
        far += x_ref[e, 8:, :] * state
        return over * state + x_ref[e, :8, :], over * adjoint + x_ref[back, 8:, :], far

    _, _, far = lax.fori_loop(0, blocks, both, (zero, zero, zero), unroll=8)
    fetch.wait()
    far = jnp.sum(far * jnp.exp(-rate), axis=1, keepdims=True) * own(norm_ref) * scale
    total = near_ref[...]
    for u in range(UNITS):
        at = sublane_of(owner, u)
        head = group * GROUP + u // 2
        value = jnp.sum(jnp.where(sub == at, far, 0.0), axis=0, keepdims=True)
        spot = POLES * lax.rem(head, 8) + 8 * (u % 2) + at
        total += jnp.where((sub == head // 8) & (lane == spot), value, 0.0)
    used = zero == 0.0
    pads = [[zero, zero], [zero, zero]]
    for u, side, line in ((6, 0, 0), (7, 0, 1), (6, 1, 2), (7, 1, None)):
        at = sub == sublane_of(owner, u)
        used = used & ~at
        if line is not None:
            for k in range(2):
                pads[k][side] = jnp.where(at, total[3 * k + line : 3 * k + line + 1], pads[k][side])

    def spare(lap, _):
        for k in range(2):
            e = 2 * lap + k
            out_ref[e, :8, :] = jnp.where(used, out_ref[e, :8, :], pads[k][0])
            out_ref[e, 8:, :] = jnp.where(used, out_ref[e, 8:, :], pads[k][1])
        return 0

    lax.fori_loop(0, blocks // 2, spare, 0, unroll=8)


def output_kernel(
    rate_ref, coef_ref, s_ref, q_ref, k_ref, v_ref, c_ref, conv_ref, grad_ref,
    mixed_ref, gq_ref, gk_ref, gv_ref, res_ref, sums,
):
    rows = q_ref.shape[0]
    spot = iota((POLES, rows), 1).astype(F32)
    sub = iota((8, WIDTH), 0)
    step = pl.program_id(0)

    @pl.when(step == 0)
    def _():
        sums[...] = jnp.zeros_like(sums)

    res = sums[...]
    for at in range(OUT_PACK):
        for u, first, line in ((6, 0, 0), (7, 0, 1), (6, 8, 2)):
            value = jnp.zeros((1, WIDTH), F32)
            for owner in range(OWNERS):
                row = first + (owner - u) % 8
                value += s_ref[(step * OUT_PACK + at) * OWNERS + owner, row : row + 1, :]
            res += jnp.where(sub == line, value, 0.0)
    sums[...] = res

    @pl.when(step == pl.num_programs(0) - 1)
    def _():
        half = HEADS // 2
        wide = iota((POLES, WIDTH), 1) % POLES == iota((POLES, WIDTH), 0)
        source = iota((WIDTH, half), 0) // POLES
        target = iota((WIDTH, half), 1)
        out = jnp.zeros((POLES, half), F32)
        for line in range(half * POLES // WIDTH):
            high, low = split(jnp.where(wide, sums[line : line + 1, :], 0.0))
            pick = jnp.where(target == 8 * line + source, 1.0, 0.0).astype(BF16)
            out += mm(high, pick) + mm(low, pick)
        res_ref[...] = out

    def batch(groups):
        heads = [(number, h, lanes_of(at, h)) for at, number in groups for h in range(GROUP)]
        tables, done = [], []
        for number, h, _ in heads:
            rate = column(rate_ref, number * GROUP + h)
            coef = column(coef_ref, number * GROUP + h)
            tables.append(
                (
                    stacked(coef * jnp.exp(-rate * (spot + 1.0)), (0, 0, 1)),
                    stacked(read_head(s_ref, number, h, 0)),
                    stacked(coef * jnp.exp(-rate * (float(rows) - spot)), (0, 0, 1)),
                    stacked(read_head(s_ref, number, h, 8)),
                )
            )
        for (inflow, state, outflow, later), (_, _, lanes) in zip(tables, heads):
            conv = conv_ref[:, lanes] + mm_tn(inflow, state)
            done.append((mixed_ref, lanes, (q_ref[:, lanes].astype(F32) * conv).astype(BF16)))
            done.append((gq_ref, lanes, (c_ref[:, lanes].astype(F32) * conv).astype(BF16)))
            grad = grad_ref[:, lanes] + mm_tn(outflow, later)
            done.append((gk_ref, lanes, (grad * v_ref[:, lanes].astype(F32)).astype(BF16)))
            done.append((gv_ref, lanes, (grad * k_ref[:, lanes].astype(F32)).astype(BF16)))
        for ref, lanes, value in done:
            ref[:, lanes] = value

    each_batch(BATCH["outputs"], batch, OUT_PACK)


def on_device(query, key_in, value, cotangent, decay_rate, residue):
    blocks = lax.axis_size("ctx") * lax.axis_size("head")
    place = lax.axis_index("ctx") * lax.axis_size("head") + lax.axis_index("head")
    rows, width = query.shape
    chunks = rows // CHUNK
    steps = GROUPS // PACK
    scale = 1.0 / math.sqrt(float(rows * blocks * WIDTH))
    rates = decay_rate.T
    norms = jnp.sqrt(-jnp.expm1(-2.0 * rates))
    coefs = residue.T * norms

    wide = pl.BlockSpec((rows, PACK * GROUP * WIDTH), lambda g: (0, g))
    thin = pl.BlockSpec((rows, OUT_PACK * GROUP * WIDTH), lambda g: (0, g))
    small = pl.BlockSpec((POLES, HEADS), lambda g: (0, 0))
    fixed = pl.BlockSpec((8, WIDTH), lambda g: (0, 0))
    tile = pl.BlockSpec((PACK * OWNERS, 16, WIDTH), lambda g: (g, 0, 0))
    part = pl.BlockSpec((PACK * GROUP, 2, chunks * POLES, WIDTH), lambda g: (g, 0, 0, 0))
    wide_bytes = 2 * rows * width
    out16 = jax.ShapeDtypeStruct((rows, width), BF16)
    out32 = jax.ShapeDtypeStruct((rows, width), F32)
    line = jax.ShapeDtypeStruct((8, WIDTH), F32)
    tiles = jax.ShapeDtypeStruct((GROUPS * OWNERS, 16, WIDTH), F32)
    part_out = jax.ShapeDtypeStruct((HEADS, 2, chunks * POLES, WIDTH), F32)

    def call(kernel, name, grid, in_specs, out_specs, out_shape, passes, limit=None, scratch=(), **fixed_args):
        return pl.pallas_call(
            functools.partial(kernel, **fixed_args),
            grid=grid,
            in_specs=in_specs,
            out_specs=out_specs,
            out_shape=out_shape,
            scratch_shapes=scratch,
            cost_estimate=pl.CostEstimate(
                flops=10**9 * passes, bytes_accessed=passes * wide_bytes, transcendentals=0
            ),
            compiler_params=pltpu.CompilerParams(vmem_limit_bytes=limit),
            name=name,
        )

    gates = (query, key_in, value, cotangent)
    states = call(states_kernel, "states", (steps,), [small, wide, wide, wide, wide], tile, tiles, 4)(rates, *gates)
    gathered = lax.all_to_all(states, ("ctx", "head"), split_axis=0, concat_axis=0, tiled=True)

    near, parts, *products = call(
        near_kernel,
        "near",
        (steps,),
        [small, small, wide, wide, wide, wide],
        [fixed, part, wide, wide, wide, wide],
        [line, part_out, out16, out16, out16, out16],
        9,
        scale=scale,
    )(rates, norms, *gates)

    conv, grad = call(
        local_kernel,
        "local",
        (steps,),
        [small, small, part, wide, wide, wide, wide],
        [wide, wide],
        [out32, out32],
        9,
        limit=LOCAL_LIMIT,
    )(rates, coefs, parts, *products)

    whole = pl.BlockSpec(memory_space=pltpu.VMEM)
    scanned = call(
        scan_kernel,
        "scan",
        (),
        [pl.BlockSpec(memory_space=pltpu.SMEM), whole, whole, pl.BlockSpec(memory_space=pltpu.HBM), whole],
        whole,
        tiles,
        1,
        limit=VMEM_LIMIT,
        scratch=[pltpu.VMEM((8, WIDTH), F32), pltpu.SemaphoreType.DMA],
        block_rows=rows,
        scale=scale,
    )(place.reshape(1), rates, norms, near, gathered)
    entering = lax.all_to_all(scanned, ("ctx", "head"), split_axis=0, concat_axis=0, tiled=True)

    *outs, res = call(
        output_kernel,
        "outputs",
        (GROUPS // OUT_PACK,),
        [small, small, whole, thin, thin, thin, thin, thin, thin],
        [thin, thin, thin, thin, pl.BlockSpec((POLES, HEADS // 2), lambda g: (0, 0))],
        [out16, out16, out16, out16, jax.ShapeDtypeStruct((POLES, HEADS // 2), F32)],
        12,
        limit=OUT_LIMIT,
        scratch=[pltpu.VMEM((8, WIDTH), F32)],
    )(rates, coefs, entering, *gates, conv, grad)
    return (*outs, res.T)


def solution(mesh):
    wide = P(("ctx", "head"), None)
    return jax.shard_map(
        on_device,
        mesh=mesh,
        in_specs=(wide, wide, wide, wide, P(), P()),
        out_specs=(wide, wide, wide, wide, P("head", None)),
        check_vma=False,
    )
```

```python
import functools
import math

import jax
import jax.numpy as jnp
from jax import lax
from jax.experimental import pallas as pl
from jax.experimental.pallas import tpu as pltpu
from jax.sharding import PartitionSpec as P

HEADS = 48
POLES = 16
WIDTH = 128
GROUP = 3
GROUPS = HEADS // GROUP
PACK = 4
OWNERS = 8
UNITS = 2 * GROUP
CHUNK = 64
BATCH = {"states": 4, "near": 4, "local": 4, "outputs": 4}
F32 = jnp.float32
BF16 = jnp.bfloat16
VMEM_LIMIT = 12 * 2**20
OUT_LIMIT = 51 * 2**20
NEAR_LIMIT = 51 * 2**20
LOCAL_LIMIT = None
OUT_PACK = 4


def split(x):
    high = x.astype(BF16)
    return high, (x - high.astype(F32)).astype(BF16)


def iota(shape, dim):
    return lax.broadcasted_iota(jnp.int32, shape, dim)


def mm(a, b):
    return jnp.dot(a, b, preferred_element_type=F32)


def mm_nt(a, b):
    return lax.dot_general(a, b, (((1,), (1,)), ((), ())), preferred_element_type=F32)


def mm_tn(a, b):
    return lax.dot_general(a, b, (((0,), (0,)), ((), ())), preferred_element_type=F32)


def stacked(x, parts=(0, 1, 0)):
    both = split(x)
    return jnp.concatenate([both[p] for p in parts], 0)


def column(table, head, first=0, count=POLES):
    hit = iota((count, HEADS), 1) == head
    return jnp.sum(jnp.where(hit, table[first : first + count, :], 0.0), axis=1, keepdims=True)


def product(a_ref, b_ref, lanes):
    return split(a_ref[:, lanes].astype(F32) * b_ref[:, lanes].astype(F32))


def lanes_of(at, h):
    return pl.ds(pl.multiple_of((at * GROUP + h) * WIDTH, WIDTH), WIDTH)


def each_batch(batch, body, pack=PACK):
    def lap(n, _):
        body([(n * batch + j, pl.program_id(0) * pack + n * batch + j) for j in range(batch)])
        return 0

    lax.fori_loop(0, pack // batch, lap, 0)


def sublane_of(owner, unit):
    return lax.rem(owner + 8 - unit, 8)


def read_unit(ref, at, u, first):
    sub = iota((8, WIDTH), 0)
    tile = jnp.zeros((8, WIDTH), F32)
    for owner in range(OWNERS):
        tile = jnp.where(sub == (owner - u) % 8, ref[at * OWNERS + owner, pl.ds(first, 8), :], tile)
    return tile


def read_head(ref, at, h, first):
    return jnp.concatenate([read_unit(ref, at, 2 * h, first), read_unit(ref, at, 2 * h + 1, first)], 0)


def states_kernel(rate_ref, q_ref, k_ref, v_ref, c_ref, out_ref):
    rows = q_ref.shape[0]
    spot = iota((POLES, rows), 1).astype(F32)
    sub = iota((8, WIDTH), 0)

    def batch(groups):
        for at, number in groups:
            ahead, back = [], []
            for h in range(GROUP):
                lanes = lanes_of(at, h)
                rate = column(rate_ref, number * GROUP + h)

                def state(weights, high, low):
                    w_hi, w_lo = split(weights)
                    both = mm(jnp.concatenate([w_hi, w_lo], 0), high)
                    return both[:POLES] + both[POLES:] + mm(w_hi, low)

                fwd = state(jnp.exp(-rate * (float(rows - 1) - spot)), *product(k_ref, v_ref, lanes))
                bwd = state(jnp.exp(-rate * spot), *product(c_ref, q_ref, lanes))
                ahead += [fwd[:8], fwd[8:]]
                back += [bwd[:8], bwd[8:]]
            for owner in range(OWNERS):
                for first, units in ((0, ahead), (8, back)):
                    tile = jnp.zeros((8, WIDTH), F32)
                    for u in range(UNITS):
                        tile = jnp.where(sub == (owner - u) % 8, units[u], tile)
                    out_ref[at * OWNERS + owner, first : first + 8, :] = tile

    each_batch(BATCH["states"], batch)


def near_kernel(
    rate_ref, norm_ref, q_ref, k_ref, v_ref, c_ref,
    out_ref, part_ref, ph_ref, pl_ref, gh_ref, gl_ref, *, scale,
):
    rows = q_ref.shape[0]
    chunks = rows // CHUNK
    step = pl.program_id(0)
    spot = iota((POLES, chunks * CHUNK), 1)
    local = (spot % CHUNK).astype(F32)
    causal = iota((CHUNK, CHUNK), 0) >= iota((CHUNK, CHUNK), 1)
    lane = iota((8, WIDTH), 1)
    sub = iota((8, WIDTH), 0)
    wide = iota((POLES, WIDTH), 1) % POLES == iota((POLES, WIDTH), 0)

    @pl.when(step == 0)
    def _():
        out_ref[...] = jnp.zeros_like(out_ref)

    def part_states(weights, high, low):
        w_hi, w_lo = split(weights)
        zero = jnp.zeros((), BF16)
        w_hi = jnp.concatenate([jnp.where(spot // CHUNK == c, w_hi, zero) for c in range(chunks)], 0)
        w_lo = jnp.concatenate([jnp.where(spot // CHUNK == c, w_lo, zero) for c in range(chunks)], 0)
        both = mm(jnp.concatenate([w_hi, w_lo], 0), high)
        return both[: chunks * POLES] + both[chunks * POLES :] + mm(w_hi, low)

    def batch(groups):
        heads = [(at * GROUP + h, number * GROUP + h, lanes_of(at, h)) for at, number in groups for h in range(GROUP)]
        crosses, moves, parts, total = [], [], [], out_ref[...]
        for at, head, lanes in heads:
            p_hi, p_lo = product(k_ref, v_ref, lanes)
            g_hi, g_lo = product(c_ref, q_ref, lanes)
            ph_ref[:, lanes], pl_ref[:, lanes] = p_hi, p_lo
            gh_ref[:, lanes], gl_ref[:, lanes] = g_hi, g_lo
            rate = column(rate_ref, head)
            f = part_states(jnp.exp(-rate * (float(CHUNK - 1) - local)), p_hi, p_lo)
            b = part_states(jnp.exp(-rate * local), g_hi, g_lo)
            part_ref[at, 0], part_ref[at, 1] = f, b
            parts.append((f, b))
            cross = jnp.zeros((2 * CHUNK, 2 * CHUNK), F32)
            for c in range(chunks):
                span = slice(c * CHUNK, (c + 1) * CHUNK)
                left = jnp.concatenate([g_hi[span], g_lo[span]], 0)
                right = jnp.concatenate([p_hi[span], p_lo[span]], 0)
                cross += mm_nt(left, right)
            cross = cross[:CHUNK, :CHUNK] + (cross[:CHUNK, CHUNK:] + cross[CHUNK:, :CHUNK])
            crosses.append(stacked(jnp.where(causal, cross, 0.0)))
        for cross, (_, head, _) in zip(crosses, heads):
            into_hi, into_lo = split(jnp.exp(-column(rate_ref, head) * local))
            moves.append(mm(jnp.where(spot // CHUNK == 2, into_lo, into_hi), cross))
        for moved, (f, b), (_, head, _) in zip(moves, parts, heads):
            rate = column(rate_ref, head)
            over = jnp.exp(-rate * float(CHUNK))
            ends = jnp.exp(-rate * (float(CHUNK - 1) - local[:, :CHUNK]))
            near = jnp.exp(rate * float(CHUNK - 1)) * jnp.sum(moved * ends, axis=1, keepdims=True)
            state = f[:POLES]
            far = jnp.zeros((POLES, WIDTH), F32)
            for c in range(1, chunks):
                far += b[c * POLES : (c + 1) * POLES] * state
                state = f[c * POLES : (c + 1) * POLES] + over * state
            near += jnp.exp(-rate) * jnp.sum(far, axis=1, keepdims=True)
            near *= column(norm_ref, head) * scale
            line = jnp.sum(jnp.where(wide, near, 0.0), axis=0, keepdims=True)
            total += jnp.where((sub == head // 8) & (lane // POLES == head % 8), line, 0.0)
        out_ref[...] = total

    each_batch(BATCH["near"], batch)


def local_kernel(rate_ref, coef_ref, part_ref, ph_ref, pl_ref, gh_ref, gl_ref, conv_ref, grad_ref):
    chunks = ph_ref.shape[0] // CHUNK
    wide = 3 * CHUNK + 3 * POLES
    lane_t = iota((POLES, wide), 1)
    hit = (lane_t - 3 * CHUNK) % POLES == iota((POLES, wide), 0)
    ramp = (lane_t % CHUNK).astype(F32)
    here = iota((POLES, CHUNK), 1).astype(F32)
    down = iota((CHUNK, wide), 0)
    lane = iota((CHUNK, wide), 1)
    low_part = ((lane >= 2 * CHUNK) & (lane < 3 * CHUNK)) | (lane >= 3 * CHUNK + 2 * POLES)

    def batch(groups):
        heads = [(at * GROUP + h, number * GROUP + h, lanes_of(at, h)) for at, number in groups for h in range(GROUP)]
        done = []
        for side, (high_ref, low_ref, out_ref) in enumerate(((ph_ref, pl_ref, conv_ref), (gh_ref, gl_ref, grad_ref))):
            flip = (lambda x: float(CHUNK - 1) - x) if side else (lambda x: x)
            keep = ((down <= lane % CHUNK) if side else (down >= lane % CHUNK)) | (lane >= 3 * CHUNK)
            tables = []
            for _, head, _ in heads:
                rate = column(rate_ref, head)
                left = column(coef_ref, head) * jnp.exp(-rate * flip(here))
                right = jnp.where(
                    lane_t < 3 * CHUNK, jnp.exp(rate * flip(ramp)), jnp.where(hit, jnp.exp(-rate), 0.0)
                )
                table = mm_tn(stacked(left, (0, 0, 1)), stacked(right))
                t_hi, t_lo = split(jnp.where(keep, table, 0.0))
                tables.append(jnp.where(low_part, t_lo, t_hi))
            for table, (at, head, lanes) in zip(tables, heads):
                over = jnp.exp(-column(rate_ref, head) * float(CHUNK))
                state = jnp.zeros((POLES, WIDTH), F32)
                for c in reversed(range(chunks)) if side else range(chunks):
                    span = slice(c * CHUNK, (c + 1) * CHUNK)
                    s_hi, s_lo = split(state)
                    high, low = high_ref[span, lanes], low_ref[span, lanes]
                    source = jnp.concatenate([high, low, high, s_hi, s_lo, s_hi], 0)
                    done.append((out_ref, span, lanes, mm(table, source)))
                    state = part_ref[at, side, c * POLES : (c + 1) * POLES] + over * state
        for out_ref, span, lanes, value in done:
            out_ref[span, lanes] = value

    each_batch(BATCH["local"], batch)


def scan_kernel(place_ref, rate_ref, norm_ref, near_hbm, x_ref, out_ref, near_ref, arrived, *, block_rows, scale):
    fetch = pltpu.make_async_copy(near_hbm, near_ref, arrived)
    fetch.start()
    blocks = x_ref.shape[0]
    group = place_ref[0] // OWNERS
    owner = lax.rem(place_ref[0], OWNERS)
    sub = iota((8, WIDTH), 0)
    lane = iota((8, WIDTH), 1)
    zero = jnp.zeros((8, WIDTH), F32)

    def own(table):
        rows = zero
        for u in range(UNITS):
            rows = jnp.where(
                sub == sublane_of(owner, u), column(table, group * GROUP + u // 2, 8 * (u % 2), 8), rows
            )
        return rows

    rate = own(rate_ref)
    over = jnp.exp(-rate * float(block_rows))

    def both(e, carry):
        state, adjoint, far = carry
        back = blocks - 1 - e
        out_ref[e, :8, :] = state
        out_ref[back, 8:, :] = adjoint
        far += x_ref[e, 8:, :] * state
        return over * state + x_ref[e, :8, :], over * adjoint + x_ref[back, 8:, :], far

    _, _, far = lax.fori_loop(0, blocks, both, (zero, zero, zero), unroll=8)
    fetch.wait()
    far = jnp.sum(far * jnp.exp(-rate), axis=1, keepdims=True) * own(norm_ref) * scale
    total = near_ref[...]
    for u in range(UNITS):
        at = sublane_of(owner, u)
        head = group * GROUP + u // 2
        value = jnp.sum(jnp.where(sub == at, far, 0.0), axis=0, keepdims=True)
        spot = POLES * lax.rem(head, 8) + 8 * (u % 2) + at
        total += jnp.where((sub == head // 8) & (lane == spot), value, 0.0)
    used = zero == 0.0
    pads = [[zero, zero], [zero, zero]]
    for u, side, line in ((6, 0, 0), (7, 0, 1), (6, 1, 2), (7, 1, None)):
        at = sub == sublane_of(owner, u)
        used = used & ~at
        if line is not None:
            for k in range(2):
                pads[k][side] = jnp.where(at, total[3 * k + line : 3 * k + line + 1], pads[k][side])

    def spare(lap, _):
        for k in range(2):
            e = 2 * lap + k
            out_ref[e, :8, :] = jnp.where(used, out_ref[e, :8, :], pads[k][0])
            out_ref[e, 8:, :] = jnp.where(used, out_ref[e, 8:, :], pads[k][1])
        return 0

    lax.fori_loop(0, blocks // 2, spare, 0, unroll=8)


def output_kernel(
    rate_ref, coef_ref, s_ref, q_ref, k_ref, v_ref, c_ref, conv_ref, grad_ref,
    mixed_ref, gq_ref, gk_ref, gv_ref, res_ref, sums,
):
    rows = q_ref.shape[0]
    spot = iota((POLES, rows), 1).astype(F32)
    sub = iota((8, WIDTH), 0)
    step = pl.program_id(0)

    @pl.when(step == 0)
    def _():
        sums[...] = jnp.zeros_like(sums)

    res = sums[...]
    for at in range(OUT_PACK):
        for u, first, line in ((6, 0, 0), (7, 0, 1), (6, 8, 2)):
            value = jnp.zeros((1, WIDTH), F32)
            for owner in range(OWNERS):
                row = first + (owner - u) % 8
                value += s_ref[(step * OUT_PACK + at) * OWNERS + owner, row : row + 1, :]
            res += jnp.where(sub == line, value, 0.0)
    sums[...] = res

    @pl.when(step == pl.num_programs(0) - 1)
    def _():
        half = HEADS // 2
        wide = iota((POLES, WIDTH), 1) % POLES == iota((POLES, WIDTH), 0)
        source = iota((WIDTH, half), 0) // POLES
        target = iota((WIDTH, half), 1)
        out = jnp.zeros((POLES, half), F32)
        for line in range(half * POLES // WIDTH):
            high, low = split(jnp.where(wide, sums[line : line + 1, :], 0.0))
            pick = jnp.where(target == 8 * line + source, 1.0, 0.0).astype(BF16)
            out += mm(high, pick) + mm(low, pick)
        res_ref[...] = out

    def batch(groups):
        heads = [(number, h, lanes_of(at, h)) for at, number in groups for h in range(GROUP)]
        tables, done = [], []
        for number, h, _ in heads:
            rate = column(rate_ref, number * GROUP + h)
            coef = column(coef_ref, number * GROUP + h)
            tables.append(
                (
                    stacked(coef * jnp.exp(-rate * (spot + 1.0)), (0, 0, 1)),
                    stacked(read_head(s_ref, number, h, 0)),
                    stacked(coef * jnp.exp(-rate * (float(rows) - spot)), (0, 0, 1)),
                    stacked(read_head(s_ref, number, h, 8)),
                )
            )
        for (inflow, state, outflow, later), (_, _, lanes) in zip(tables, heads):
            conv = conv_ref[:, lanes] + mm_tn(inflow, state)
            done.append((mixed_ref, lanes, (q_ref[:, lanes].astype(F32) * conv).astype(BF16)))
            done.append((gq_ref, lanes, (c_ref[:, lanes].astype(F32) * conv).astype(BF16)))
            grad = grad_ref[:, lanes] + mm_tn(outflow, later)
            done.append((gk_ref, lanes, (grad * v_ref[:, lanes].astype(F32)).astype(BF16)))
            done.append((gv_ref, lanes, (grad * k_ref[:, lanes].astype(F32)).astype(BF16)))
        for ref, lanes, value in done:
            ref[:, lanes] = value

    each_batch(BATCH["outputs"], batch, OUT_PACK)


def on_device(query, key_in, value, cotangent, decay_rate, residue):
    blocks = lax.axis_size("ctx") * lax.axis_size("head")
    place = lax.axis_index("ctx") * lax.axis_size("head") + lax.axis_index("head")
    rows, width = query.shape
    chunks = rows // CHUNK
    steps = GROUPS // PACK
    scale = 1.0 / math.sqrt(float(rows * blocks * WIDTH))
    rates = decay_rate.T
    norms = jnp.sqrt(-jnp.expm1(-2.0 * rates))
    coefs = residue.T * norms

    wide = pl.BlockSpec((rows, PACK * GROUP * WIDTH), lambda g: (0, g))
    thin = pl.BlockSpec((rows, OUT_PACK * GROUP * WIDTH), lambda g: (0, g))
    small = pl.BlockSpec((POLES, HEADS), lambda g: (0, 0))
    fixed = pl.BlockSpec((8, WIDTH), lambda g: (0, 0))
    tile = pl.BlockSpec((PACK * OWNERS, 16, WIDTH), lambda g: (g, 0, 0))
    part = pl.BlockSpec((PACK * GROUP, 2, chunks * POLES, WIDTH), lambda g: (g, 0, 0, 0))
    wide_bytes = 2 * rows * width
    out16 = jax.ShapeDtypeStruct((rows, width), BF16)
    out32 = jax.ShapeDtypeStruct((rows, width), F32)
    line = jax.ShapeDtypeStruct((8, WIDTH), F32)
    tiles = jax.ShapeDtypeStruct((GROUPS * OWNERS, 16, WIDTH), F32)
    part_out = jax.ShapeDtypeStruct((HEADS, 2, chunks * POLES, WIDTH), F32)

    def call(kernel, name, grid, in_specs, out_specs, out_shape, passes, limit=None, scratch=(), **fixed_args):
        return pl.pallas_call(
            functools.partial(kernel, **fixed_args),
            grid=grid,
            in_specs=in_specs,
            out_specs=out_specs,
            out_shape=out_shape,
            scratch_shapes=scratch,
            cost_estimate=pl.CostEstimate(
                flops=10**9 * passes, bytes_accessed=passes * wide_bytes, transcendentals=0
            ),
            compiler_params=pltpu.CompilerParams(vmem_limit_bytes=limit),
            name=name,
        )

    gates = (query, key_in, value, cotangent)
    states = call(states_kernel, "states", (steps,), [small, wide, wide, wide, wide], tile, tiles, 4)(rates, *gates)
    gathered = lax.all_to_all(states, ("ctx", "head"), split_axis=0, concat_axis=0, tiled=True)

    near, parts, *products = call(
        near_kernel,
        "near",
        (steps,),
        [small, small, wide, wide, wide, wide],
        [fixed, part, wide, wide, wide, wide],
        [line, part_out, out16, out16, out16, out16],
        9,
        limit=NEAR_LIMIT,
        scale=scale,
    )(rates, norms, *gates)

    conv, grad = call(
        local_kernel,
        "local",
        (steps,),
        [small, small, part, wide, wide, wide, wide],
        [wide, wide],
        [out32, out32],
        9,
        limit=LOCAL_LIMIT,
    )(rates, coefs, parts, *products)

    whole = pl.BlockSpec(memory_space=pltpu.VMEM)
    scanned = call(
        scan_kernel,
        "scan",
        (),
        [pl.BlockSpec(memory_space=pltpu.SMEM), whole, whole, pl.BlockSpec(memory_space=pltpu.HBM), whole],
        whole,
        tiles,
        1,
        limit=VMEM_LIMIT,
        scratch=[pltpu.VMEM((8, WIDTH), F32), pltpu.SemaphoreType.DMA],
        block_rows=rows,
        scale=scale,
    )(place.reshape(1), rates, norms, near, gathered)
    entering = lax.all_to_all(scanned, ("ctx", "head"), split_axis=0, concat_axis=0, tiled=True)

    *outs, res = call(
        output_kernel,
        "outputs",
        (GROUPS // OUT_PACK,),
        [small, small, whole, thin, thin, thin, thin, thin, thin],
        [thin, thin, thin, thin, pl.BlockSpec((POLES, HEADS // 2), lambda g: (0, 0))],
        [out16, out16, out16, out16, jax.ShapeDtypeStruct((POLES, HEADS // 2), F32)],
        12,
        limit=OUT_LIMIT,
        scratch=[pltpu.VMEM((8, WIDTH), F32)],
    )(rates, coefs, entering, *gates, conv, grad)
    return (*outs, res.T)


def solution(mesh):
    wide = P(("ctx", "head"), None)
    return jax.shard_map(
        on_device,
        mesh=mesh,
        in_specs=(wide, wide, wide, wide, P(), P()),
        out_specs=(wide, wide, wide, wide, P("head", None)),
        check_vma=False,
    )
```
